256 devices in a mesh: gx: 16 (over y, z_hi, core), gy: 16 (over z_lo, x).
Axes of the slice: x: 4, y: 4, z: 8 (z_hi: 2, z_lo: 4; z = z_hi * 4 + z_lo), core: 2. Of those that a mesh axis runs over, the one named last changes fastest.
Arguments:
- pressure: float32 [512, 512, 128], P('gx', 'gy'), may hold values from -6 to 6
- vel_x: float32 [512, 512, 128], P('gx', 'gy'), may hold values from -6 to 6
- vel_y: float32 [512, 512, 128], P('gx', 'gy'), may hold values from -6 to 6
- vel_z: float32 [512, 512, 128], P('gx', 'gy'), may hold values from -6 to 6
- material: int32 [512, 512, 128], P('gx', 'gy'), may hold values from 0 to 3
- density_table: float32 [4], replicated, may hold values from 0.5 to 4
- speed_table: float32 [4], replicated, may hold values from 0.3 to 1
- panel_vals: float32 [512, 128, 8, 128], P(('gx', 'gy')), may hold values from -6 to 6
- panel_tile: int32 [512, 128, 1], P(('gx', 'gy')), may hold values from 0 to 255; in each aligned block of 256 rows (0 to 255, 256 to 511, ..., all dimensions but the last counted through in order) at most 2 rows name the same one
- panel_cell: int32 [512, 128], P(('gx', 'gy')), may hold values from 0 to 1023
Outputs:
- pressure_out: float32 [512, 512, 128], P('gx', 'gy')
- vel_x_out: float32 [512, 512, 128], P('gx', 'gy')
- vel_y_out: float32 [512, 512, 128], P('gx', 'gy')
- vel_z_out: float32 [512, 512, 128], P('gx', 'gy')
The draws below stay inside these ranges and needn't reach their ends.
Inputs may be any that keep to these rules, and one draw needn't show every extreme that they name: `panel_tile`: among the 256 columns of the panels of one device, no tile is named more than 2 times, a bound that some block reaches.
All inputs are finite; a program needn't handle non-finite values.
Results may differ from the reference program's by a relative error of at most 0.00002.
Values sent between devices are 32-bit elements; how exact they have to be, the bound alone decides.
No kernel may reach another device: no remote copies, remote signals or barrier semaphores. Data moves between devices by JAX's collectives and lax.ppermute only.
A program may use at most 64 MiB of HBM per device.

```python
import math
import jax
import jax.numpy as jnp
import numpy as np

CX = 32
CY = 32
NZ = 128
PW = 128
PAN_DEV = 2
STEPS = 8
NMAT = 4
NX = 512
NY = 512
NPAN = 512
CAP = 2
N_GY = 16
DEVICES = 256


def touch_ends(values, key, low, top_value):
    shape = values.shape
    spot = [jax.random.randint(jax.random.fold_in(key, axis), (), 0, shape[axis]) for axis in range(len(shape))]
    values = values.at[tuple(spot)].set(low)
    longest = shape.index(max(shape))
    spot[longest] = (spot[longest] + 1) % shape[longest]
    return values.at[tuple(spot)].set(top_value)


def level_of(key, dims, pieces, smallest, largest):
    def one(position, shards_of):
        heights = jax.random.uniform(jax.random.fold_in(jax.random.fold_in(key, 6), position), (shards_of,), jnp.float32, smallest / len(pieces), largest / len(pieces))
        return jnp.repeat(jnp.exp(heights), dims[position] // shards_of).reshape((-1,) + (1,) * (len(dims) - position - 1))

    gain = one(*pieces[0])
    for cut in pieces[1:]:
        gain = gain * one(*cut)
    return gain


def assign_block(stream_key, own, number, rows, number_of, top, reach, skew):
    sequence = jax.random.permutation(stream_key, number_of)
    packed, usual = load_shares(number_of, rows * top, reach, skew, True), load_shares(number_of, rows * top, reach, skew, False)
    places = jnp.arange(number_of)

    def named(lengths, offset_by):
        used = int((lengths > 0).sum())
        fixed = max(1, used // 4)
        shifted = fixed + (places - fixed + offset_by * (used - fixed)) % max(1, number_of - fixed)
        return jnp.zeros((number_of,), jnp.int32).at[sequence[jnp.where(places < fixed, places, shifted)]].set(jnp.asarray(lengths, jnp.int32))

    lengths = jnp.where(number % 4 == 0, named(packed, number // 4), named(usual, number - number // 4 - 1))
    mixed = jax.random.permutation(jax.random.fold_in(own, 3), number_of)
    source_of, sink = mixed[0:number_of // 2 * 2:2], mixed[1:number_of // 2 * 2:2]
    margin = jnp.minimum(lengths[source_of] - 1, reach - lengths[sink]) // 2
    margin = jnp.where((source_of == sequence[0]) | (sink == sequence[0]) | (lengths[sink] == 0), 0, jnp.maximum(margin, 0))
    shifted = jax.random.randint(jax.random.fold_in(own, 4), (number_of // 2,), 0, 1 << 20) % (margin + 1)
    lengths = lengths.at[source_of].add(-shifted).at[sink].add(shifted)
    labels = jnp.searchsorted(jnp.cumsum(lengths), jnp.arange(rows * top), side="right").astype(jnp.int32)
    listing = labels.reshape(top, rows).T
    listing = listing[jax.random.permutation(jax.random.fold_in(own, 1), rows)]
    offset_by = jax.random.randint(jax.random.fold_in(own, 2), (rows, 1), 0, top)
    return jnp.take_along_axis(listing, (jnp.arange(top)[None, :] + offset_by) % top, axis=1)


def load_shares(count, total, limit, slope, full):
    portions = [(1 << 20) // math.isqrt(grade ** slope) + 1 for grade in range(1, count + 1)]
    largest = limit if full else min(limit, max(-(-total // count), total * portions[0] // sum(portions)))
    least = 1 if total - largest >= count - 1 else 0
    given, rest = [largest] + [least] * (count - 1), total - largest - least * (count - 1)
    while rest > 0:
        free = [i for i in range(1, count) if given[i] < largest] or [i for i in range(1, count) if given[i] < limit]
        mass, left = sum([portions[i] for i in free]), rest
        for i in free:
            extra = min(limit - given[i], max(1, left * portions[i] // mass), rest)
            given[i] = given[i] + extra
            rest = rest - extra
    return np.array(given)


def gaussian(key, dims, scale, bound, cuts=(), kind=jnp.bfloat16):
    drawn = jax.random.normal(key, dims, jnp.float32) * scale
    if len(cuts) > 0:
        drawn = level_of(key, dims, cuts, -0.22, 0.18) * drawn
    return jnp.clip(drawn, min=-bound, max=bound).astype(kind)


def setup_inputs(seed: int = 0) -> dict:
    key_list = jax.random.split(jax.random.key(seed), 11)
    pressure = gaussian(key_list[0], (NX, NY, NZ), 1.0, 6.0, ((0, 16), (1, 16)), jnp.float32)
    vel_x = gaussian(key_list[1], (NX, NY, NZ), 1.0, 6.0, ((0, 16), (1, 16)), jnp.float32)
    vel_y = gaussian(key_list[2], (NX, NY, NZ), 1.0, 6.0, ((0, 16), (1, 16)), jnp.float32)
    vel_z = gaussian(key_list[3], (NX, NY, NZ), 1.0, 6.0, ((0, 16), (1, 16)), jnp.float32)
    material = touch_ends(jax.random.randint(key_list[4], (NX, NY, NZ), 0, NMAT), jax.random.fold_in(key_list[4], 1), 0, NMAT - 1).astype(jnp.int32)
    density_table = jnp.clip(jnp.exp(jax.random.uniform(key_list[5], (NMAT,), jnp.float32, math.log(0.5), math.log(4.0))), 0.5, 4.0)
    speed_table = jnp.clip(jax.random.uniform(key_list[6], (NMAT,), jnp.float32, 0.3, 1.0), 0.3, 1.0)
    panel_vals = gaussian(key_list[7], (NPAN, PW, STEPS, NZ), 1.0, 6.0, ((0, 256),), jnp.float32)
    panel_tile_keys = jax.random.split(jax.random.fold_in(key_list[8], 1), NPAN * PW // (PAN_DEV * PW))
    panel_tile_turns = jax.random.permutation(jax.random.fold_in(key_list[8], 3), NPAN * PW // (PAN_DEV * PW))
    panel_tile = jax.vmap(lambda own, number: assign_block(jax.random.fold_in(key_list[8], 2), own, number, PAN_DEV * PW, DEVICES, 1, CAP, 2))(panel_tile_keys, panel_tile_turns).reshape((NPAN, PW, 1))
    panel_cell = touch_ends(jax.random.randint(key_list[9], (NPAN, PW), 0, CX * CY), jax.random.fold_in(key_list[9], 1), 0, (CX * CY) - 1).astype(jnp.int32)
    return dict(pressure=pressure, vel_x=vel_x, vel_y=vel_y, vel_z=vel_z, material=material, density_table=density_table, speed_table=speed_table, panel_vals=panel_vals, panel_tile=panel_tile, panel_cell=panel_cell)


courant = 0.55


def lookup(material, table):
    total = jnp.zeros(material.shape, jnp.float32)
    for index in range(NMAT):
        total = total + jnp.where(material == index, table[index], 0.0)
    return total


def next_along(field, axis):
    size = field.shape[axis]
    inner = jax.lax.slice_in_dim(field, 1, size, axis=axis)
    zero_plane = jnp.zeros_like(jax.lax.slice_in_dim(field, 0, 1, axis=axis))
    return jnp.concatenate([inner, zero_plane], axis=axis)


def prev_along(field, axis):
    size = field.shape[axis]
    inner = jax.lax.slice_in_dim(field, 0, size - 1, axis=axis)
    zero_plane = jnp.zeros_like(jax.lax.slice_in_dim(field, 0, 1, axis=axis))
    return jnp.concatenate([zero_plane, inner], axis=axis)


def reference(pressure, vel_x, vel_y, vel_z, material, density_table, speed_table, panel_vals, panel_tile, panel_cell):
    density = lookup(material, density_table)
    speed = lookup(material, speed_table)
    buoyancy = 1.0 / density
    stiffness = density * speed * speed
    target = panel_tile.reshape(-1).astype(jnp.int32)
    cell_index = panel_cell.reshape(-1).astype(jnp.int32)
    xs_global = (target // N_GY) * CX + cell_index // CY
    ys_global = (target % N_GY) * CY + cell_index % CY
    values = panel_vals.reshape(-1, STEPS, NZ)
    for step in range(STEPS):
        vel_x = vel_x - courant * buoyancy * (next_along(pressure, 0) - pressure)
        vel_y = vel_y - courant * buoyancy * (next_along(pressure, 1) - pressure)
        vel_z = vel_z - courant * buoyancy * (next_along(pressure, 2) - pressure)
        divergence = (vel_x - prev_along(vel_x, 0)) + (vel_y - prev_along(vel_y, 1))
        divergence = divergence + (vel_z - prev_along(vel_z, 2))
        source = jnp.zeros(pressure.shape, pressure.dtype).at[xs_global, ys_global].add(values[:, step, :])
        pressure = pressure - courant * stiffness * divergence + courant * stiffness * source
    return pressure, vel_x, vel_y, vel_z
```

```python
import jax
import jax.numpy as jnp
from jax import lax
from jax.experimental import pallas as pl
from jax.experimental.pallas import tpu as pltpu
from jax.sharding import PartitionSpec as P

courant = 0.55
STEPS = 8
DEPTH = 8
LAST = STEPS - 1
X_START = [sum(LAST - t for t in range(s)) for s in range(STEPS)]
X_PLANES = X_START[LAST]
PAIRS = 4
Y_REACH = [LAST - 1 - q for q in range(PAIRS)]
VMEM = pl.BlockSpec(memory_space=pltpu.VMEM)
SMEM = pl.BlockSpec(memory_space=pltpu.SMEM)


def call(kernel, outs, in_specs, micros, mib, scratch=()):
    return pl.pallas_call(
        kernel,
        out_shape=[jax.ShapeDtypeStruct(shape, jnp.float32) for shape in outs],
        in_specs=in_specs,
        out_specs=[VMEM] * len(outs),
        scratch_shapes=list(scratch),
        compiler_params=pltpu.CompilerParams(vmem_limit_bytes=mib << 20),
        cost_estimate=pl.CostEstimate(
            flops=0, transcendentals=0, bytes_accessed=int(micros * 2_000_000)
        ),
    )


def moved(block, axis, distance):
    devices = range(lax.axis_size(axis))
    route = [(i - distance, i) for i in devices if i - distance in devices]
    return lax.ppermute(block, axis, route)


def pack_kernel(p, vx, vy, vz, mat, first, last):
    wide = p.shape[0]
    for a, ref in enumerate((p, vx, vy, vz)):
        first[a] = ref[:DEPTH]
        last[a] = ref[wide - DEPTH :]
    first[4] = mat[:DEPTH].astype(jnp.float32) + 1.0
    last[4] = mat[wide - DEPTH :].astype(jnp.float32) + 1.0


def send_kernel(tile, rank, cell, vals, out):
    block = 2 * STEPS + 1
    tiles = out.shape[0] // block
    zero = jnp.zeros((16, out.shape[1]), jnp.float32)
    lane = lax.broadcasted_iota(jnp.int32, (1, out.shape[1]), 1)

    def clear(i, c):
        for u in range(4):
            out[pl.ds(pl.multiple_of(i * 64 + u * 16, 16), 16), :] = zero
        return c

    lax.fori_loop(0, out.shape[0] // 64, clear, 0)
    out[pl.ds(2 * STEPS, tiles, stride=block), :] = jnp.full((tiles, out.shape[1]), 65536.0)

    def place(i, c):
        for u in range(8):
            k = i * 8 + u
            at = tile[k] * block
            slot = rank[k]
            out[pl.ds(at + slot * STEPS, STEPS), :] = vals[k]
            named = out[pl.ds(at + 2 * STEPS, 1), :]
            own = cell[k].astype(jnp.float32)
            out[pl.ds(at + 2 * STEPS, 1), :] = jnp.where(lane == slot, own, named)
        return c

    lax.fori_loop(0, vals.shape[0] // 8, place, 0)


def edge_kernel(p, vx, vy, vz, mat, low, high, first, last):
    wide, tall = p.shape[:2]
    for a, ref in enumerate((p, vx, vy, vz, mat)):
        for out, rows in ((first, slice(0, 8)), (last, slice(tall - 8, tall))):
            out[a, :DEPTH] = low[a, :, rows, :]
            inner = ref[:, rows, :]
            if a == 4:
                inner = inner.astype(jnp.float32) + 1.0
            out[a, DEPTH : DEPTH + wide] = inner
            out[a, DEPTH + wide :] = high[a, :, rows, :]


def extend_kernel(btab, stab, p, vx, vy, vz, mat, low, high, ylow, yhigh, *outs):
    wide, _ = p.shape[:2]

    def put(x, a, parts):
        full = jnp.concatenate(parts, axis=0)
        if a < 4:
            outs[a][x] = full
            return
        b = jnp.zeros_like(full)
        s = jnp.zeros_like(full)
        for m in range(btab.shape[0]):
            b = jnp.where(full == float(m + 1), btab[m], b)
            s = jnp.where(full == float(m + 1), stab[m], s)
        outs[4][x] = b
        outs[5][x] = s

    for a, ref in enumerate((p, vx, vy, vz, mat)):

        def lower(i, c):
            put(i, a, [ylow[a, i], low[a, i], yhigh[a, i]])
            return c

        def inner(i, c):
            mid = ref[i]
            if a == 4:
                mid = mid.astype(jnp.float32) + 1.0
            put(i + DEPTH, a, [ylow[a, i + DEPTH], mid, yhigh[a, i + DEPTH]])
            return c

        def upper(i, c):
            x = i + DEPTH + wide
            put(x, a, [ylow[a, x], high[a, i], yhigh[a, x]])
            return c

        lax.fori_loop(0, DEPTH, lower, 0)
        lax.fori_loop(0, wide, inner, 0)
        lax.fori_loop(0, DEPTH, upper, 0)


def thirds(v):
    hi = v.astype(jnp.bfloat16)
    rest = v - hi.astype(jnp.float32)
    mid = rest.astype(jnp.bfloat16)
    return hi, mid, (rest - mid.astype(jnp.float32)).astype(jnp.bfloat16)


def one_hot(cells, base, count):
    ids = lax.broadcasted_iota(jnp.int32, (count, cells.shape[1]), 0) + base
    return jnp.where(ids.astype(jnp.float32) == cells, 1.0, 0.0).astype(jnp.bfloat16)


def spread(hot, parts):
    total = jnp.dot(hot, parts[0], preferred_element_type=jnp.float32)
    total = total + jnp.dot(hot, parts[1], preferred_element_type=jnp.float32)
    return total + jnp.dot(hot, parts[2], preferred_element_type=jnp.float32)


def source_kernel(arrived, src, first, last, parts_ref):
    block = 2 * STEPS + 1
    tiles = arrived.shape[0] // block
    wide, tall, layers = src.shape[1:]
    named = jnp.transpose(arrived[pl.ds(2 * STEPS, tiles, stride=block), :])
    cells = jnp.concatenate([named[0:1], named[1:2]], axis=1)
    for s in range(STEPS):
        for r in range(2):
            rows = pl.ds(r * STEPS + s, tiles, stride=block)
            for n, part in enumerate(thirds(arrived[rows, :])):
                parts_ref[n, r * tiles : (r + 1) * tiles, s * layers : (s + 1) * layers] = part
    chunk = 8

    def body(i, c):
        hot = one_hot(cells, i * (chunk * tall), chunk * tall)
        for s in range(0, STEPS, 2):
            span = slice(s * layers, (s + 2) * layers)
            got = spread(hot, [parts_ref[n, :, span] for n in range(3)])
            for m in range(2):
                piece = got[:, m * layers : (m + 1) * layers]
                src[s + m, pl.ds(i * chunk, chunk)] = piece.reshape(chunk, tall, layers)
        return c

    lax.fori_loop(0, wide // chunk, body, 0)
    for s in range(LAST):
        for d in range(1, LAST - s + 1):
            first[X_START[s] + d - 1] = src[s, d - 1]
            last[X_START[s] + d - 1] = src[s, wide - d]


def y_start(q, wide):
    return sum(wide + 2 * Y_REACH[t] for t in range(q))


def source_edge_kernel(src, low, high, first, last):
    wide, tall, layers = src.shape[1:]
    row = lax.broadcasted_iota(jnp.int32, (8, layers), 0)
    for q in range(PAIRS):
        near, far, reach = q, LAST - 1 - q, Y_REACH[q]
        base = y_start(q, wide)

        def pack(out, slot, a, b, is_first):
            if b is None:
                out[slot] = a
            elif is_first:
                out[slot] = jnp.where(row <= LAST - 1 - q, a, pltpu.roll(b, LAST - q, 0))
            else:
                out[slot] = jnp.where(row >= q + 1, a, pltpu.roll(b, q + 1, 0))

        for out, at, is_first in ((first, 0, True), (last, tall - 8, False)):
            rows = slice(at, at + 8)

            def inner(i, c):
                for u in range(4):
                    x = i * 4 + u
                    b = src[far, x, rows, :] if far != near else None
                    pack(out, base + reach + x, src[near, x, rows, :], b, is_first)
                return c

            lax.fori_loop(0, wide // 4, inner, 0)
            for d in range(1, reach + 1):
                with_far = far != near and d <= q
                for halo, slot in ((low, base + reach - d), (high, base + reach + wide + d - 1)):
                    a = halo[X_START[near] + d - 1, rows, :]
                    b = halo[X_START[far] + d - 1, rows, :] if with_far else None
                    pack(out, slot, a, b, is_first)


def step_kernel(
    p0, vx0, vy0, vz0, bb, ss, src, low, high, ylow, yhigh,
    p_out, vx_out, vy_out, vz_out, p, vx, vy, vz,
):
    wide, tall, layers = p_out.shape
    full = tall + 2 * DEPTH
    lane = lax.broadcasted_iota(jnp.int32, (full, layers), 1)
    blank = jnp.zeros((8, layers), jnp.float32)

    for s in range(STEPS):
        depth = LAST - s
        p_in, vx_in, vy_in, vz_in = (p0, vx0, vy0, vz0) if s == 0 else (p, vx, vy, vz)
        q = min(s, LAST - 1 - s)

        def tiles(x):
            slot = y_start(q, wide) + Y_REACH[q] + x
            lo, hi = ylow[slot], yhigh[slot]
            if s > LAST - 1 - s:
                lo, hi = pltpu.roll(lo, LAST - q, 0), pltpu.roll(hi, q + 1, 0)
            return lo, hi

        def row(i, carry, source):
            p_cur, vx_prev = carry
            p_next = p_in[i + 1]
            b = bb[i]
            vx_new = vx_in[i] - b * (p_next - p_cur)
            vy_new = vy_in[i] - b * (pltpu.roll(p_cur, full - 1, 0) - p_cur)
            up = jnp.where(lane == layers - 1, 0.0, pltpu.roll(p_cur, layers - 1, 1))
            vz_new = vz_in[i] - b * (up - p_cur)
            down = jnp.where(lane == 0, 0.0, pltpu.roll(vz_new, 1, 1))
            div = (vx_new - vx_prev) + (vy_new - pltpu.roll(vy_new, 1, 0)) + (vz_new - down)
            p_new = p_cur + ss[i] * (source - div)
            if s == LAST:
                keep = slice(DEPTH, DEPTH + tall)
                p_out[i - DEPTH] = p_new[keep]
                vx_out[i - DEPTH] = vx_new[keep]
                vy_out[i - DEPTH] = vy_new[keep]
                vz_out[i - DEPTH] = vz_new[keep]
            else:
                p[i] = p_new
                vx[i] = vx_new
                vy[i] = vy_new
                vz[i] = vz_new
            return p_next, vx_new

        begin = DEPTH - depth
        p_cur = p_in[begin]
        before = p_in[begin - 1]
        carry = (p_cur, vx_in[begin - 1] - bb[begin - 1] * (p_cur - before))
        for d in range(depth, 0, -1):
            lo, hi = tiles(-d) if d < depth else (blank, blank)
            source = jnp.concatenate([lo, low[X_START[s] + d - 1], hi], axis=0)
            carry = row(DEPTH - d, carry, source)

        def inner(n, carry):
            for u in range(4):
                i = n * 4 + u
                if s == LAST:
                    source = jnp.concatenate([blank, src[s, i], blank], axis=0)
                else:
                    lo, hi = tiles(i)
                    source = jnp.concatenate([lo, src[s, i], hi], axis=0)
                carry = row(i + DEPTH, carry, source)
            return carry

        carry = lax.fori_loop(0, wide // 4, inner, carry)
        for d in range(1, depth + 1):
            lo, hi = tiles(wide + d - 1) if d < depth else (blank, blank)
            source = jnp.concatenate([lo, high[X_START[s] + d - 1], hi], axis=0)
            carry = row(DEPTH + wide + d - 1, carry, source)


def program(
    pressure, vel_x, vel_y, vel_z, material, density_table, speed_table,
    panel_vals, panel_tile, panel_cell,
):
    devices = lax.axis_size("gx") * lax.axis_size("gy")
    wide, tall, layers = pressure.shape
    columns = panel_vals.shape[0] * panel_vals.shape[1]
    target = panel_tile.reshape(-1)
    order = jnp.arange(columns, dtype=jnp.int32)
    earlier = (target[:, None] == target[None, :]) & (order[None, :] < order[:, None])
    rank = jnp.sum(earlier.astype(jnp.int32), axis=1)
    values = panel_vals.reshape(columns, STEPS, layers)
    state = (pressure, vel_x, vel_y, vel_z, material)

    first, last = call(pack_kernel, [(5, DEPTH, tall, layers)] * 2, [VMEM] * 5, 1, 8)(*state)
    low, high = moved(last, "gx", 1), moved(first, "gx", -1)
    block = 2 * STEPS + 1
    (outgoing,) = call(
        send_kernel, [(devices * block, layers)], [SMEM] * 3 + [VMEM], 3, 12
    )(target, rank, panel_cell.reshape(-1), values)
    arrived = lax.all_to_all(
        outgoing.reshape(devices, block, 1, layers),
        ("gx", "gy"),
        split_axis=0,
        concat_axis=0,
        tiled=True,
    ).reshape(devices * block, layers)
    y_first, y_last = call(
        edge_kernel, [(5, wide + 2 * DEPTH, 8, layers)] * 2, [VMEM] * 7, 2, 12
    )(*state, low, high)
    y_low, y_high = moved(y_last, "gy", 1), moved(y_first, "gy", -1)
    b_table = courant * (1.0 / density_table)
    s_table = courant * (density_table * speed_table * speed_table)
    box = (wide + 2 * DEPTH, tall + 2 * DEPTH, layers)
    extended = call(extend_kernel, [box] * 6, [SMEM] * 2 + [VMEM] * 9, 4, 20)(
        b_table, s_table, *state, low, high, y_low, y_high
    )

    src, s_first, s_last = call(
        source_kernel,
        [(STEPS, wide, tall, layers)] + [(X_PLANES, tall, layers)] * 2,
        [VMEM],
        5,
        26,
        [pltpu.VMEM((3, 2 * devices, STEPS * layers), jnp.bfloat16)],
    )(arrived)
    s_low, s_high = moved(s_last, "gx", 1), moved(s_first, "gx", -1)
    tiles = y_start(PAIRS, wide)
    e_first, e_last = call(
        source_edge_kernel, [(tiles, 8, layers)] * 2, [VMEM] * 3, 2, 12
    )(src, s_low, s_high)
    e_low, e_high = moved(e_last, "gy", 1), moved(e_first, "gy", -1)

    return tuple(
        call(
            step_kernel,
            [(wide, tall, layers)] * 4,
            [VMEM] * 11,
            12,
            32,
            [pltpu.VMEM(box, jnp.float32)] * 4,
        )(*extended, src, s_low, s_high, e_low, e_high)
    )


def solution(mesh):
    tile = P("gx", "gy", None)
    return jax.shard_map(
        program,
        mesh=mesh,
        in_specs=(tile,) * 5
        + (
            P(),
            P(),
            P(("gx", "gy"), None, None, None),
            P(("gx", "gy"), None, None),
            P(("gx", "gy"), None),
        ),
        out_specs=(tile,) * 4,
        check_vma=False,
    )
```

```python
import jax
import jax.numpy as jnp
from jax import lax
from jax.experimental import pallas as pl
from jax.experimental.pallas import tpu as pltpu
from jax.sharding import PartitionSpec as P

courant = 0.55
STEPS = 8
DEPTH = 8
LAST = STEPS - 1
X_START = [sum(LAST - t for t in range(s)) for s in range(STEPS)]
X_PLANES = X_START[LAST]
PAIRS = 4
Y_REACH = [LAST - 1 - q for q in range(PAIRS)]
VMEM = pl.BlockSpec(memory_space=pltpu.VMEM)
SMEM = pl.BlockSpec(memory_space=pltpu.SMEM)


def call(kernel, outs, in_specs, micros, mib, scratch=()):
    return pl.pallas_call(
        kernel,
        out_shape=[
            shape
            if isinstance(shape, jax.ShapeDtypeStruct)
            else jax.ShapeDtypeStruct(shape, jnp.float32)
            for shape in outs
        ],
        in_specs=in_specs,
        out_specs=[VMEM] * len(outs),
        scratch_shapes=list(scratch),
        compiler_params=pltpu.CompilerParams(vmem_limit_bytes=mib << 20),
        cost_estimate=pl.CostEstimate(
            flops=0, transcendentals=0, bytes_accessed=int(micros * 2_000_000)
        ),
    )


def moved(block, axis, distance):
    devices = range(lax.axis_size(axis))
    route = [(i - distance, i) for i in devices if i - distance in devices]
    return lax.ppermute(block, axis, route)


def pack_kernel(p, vx, vy, vz, mat, first, last, ends, sems):
    wide = p.shape[0]
    sides = (slice(0, DEPTH), slice(wide - DEPTH, wide))
    copies = []
    for a, ref in enumerate((p, vx, vy, vz, mat)):
        for side, out in enumerate((first, last)):
            target = out.at[a] if a < 4 else ends.at[side]
            copies.append(pltpu.make_async_copy(ref.at[sides[side]], target, sems.at[a, side]))
    for copy in copies:
        copy.start()
    for copy in copies:
        copy.wait()
    first[4] = ends[0].astype(jnp.float32) + 1.0
    last[4] = ends[1].astype(jnp.float32) + 1.0


def send_kernel(tile, rank, cell, vals, out):
    block = 2 * STEPS + 1
    tiles = out.shape[0] // block
    zero = jnp.zeros((16, out.shape[1]), jnp.float32)
    lane = lax.broadcasted_iota(jnp.int32, (1, out.shape[1]), 1)

    def clear(i, c):
        for u in range(4):
            out[pl.ds(pl.multiple_of(i * 64 + u * 16, 16), 16), :] = zero
        return c

    lax.fori_loop(0, out.shape[0] // 64, clear, 0)
    out[pl.ds(2 * STEPS, tiles, stride=block), :] = jnp.full((tiles, out.shape[1]), 65536.0)

    def place(i, c):
        for u in range(8):
            k = i * 8 + u
            at = tile[k] * block
            slot = rank[k]
            out[pl.ds(at + slot * STEPS, STEPS), :] = vals[k]
            named = out[pl.ds(at + 2 * STEPS, 1), :]
            own = cell[k].astype(jnp.float32)
            out[pl.ds(at + 2 * STEPS, 1), :] = jnp.where(lane == slot, own, named)
        return c

    lax.fori_loop(0, vals.shape[0] // 8, place, 0)


def edge_kernel(p, vx, vy, vz, mat, low, high, first, last):
    wide, tall = p.shape[:2]
    for a, ref in enumerate((p, vx, vy, vz, mat)):
        for out, rows in ((first, slice(0, 8)), (last, slice(tall - 8, tall))):
            out[a, :DEPTH] = low[a, :, rows, :]
            inner = ref[:, rows, :]
            if a == 4:
                inner = inner.astype(jnp.float32) + 1.0
            out[a, DEPTH : DEPTH + wide] = inner
            out[a, DEPTH + wide :] = high[a, :, rows, :]


def extend_kernel(btab, stab, p, vx, vy, vz, mat, low, high, ylow, yhigh, *outs):
    wide, _ = p.shape[:2]

    def put(x, a, parts):
        full = jnp.concatenate(parts, axis=0)
        if a < 4:
            outs[a][x] = full
            return
        b = jnp.zeros_like(full)
        s = jnp.zeros_like(full)
        for m in range(btab.shape[0]):
            b = jnp.where(full == float(m + 1), btab[m], b)
            s = jnp.where(full == float(m + 1), stab[m], s)
        outs[4][x] = b
        outs[5][x] = s

    for a, ref in enumerate((p, vx, vy, vz, mat)):

        def lower(i, c):
            put(i, a, [ylow[a, i], low[a, i], yhigh[a, i]])
            return c

        def inner(i, c):
            mid = ref[i]
            if a == 4:
                mid = mid.astype(jnp.float32) + 1.0
            put(i + DEPTH, a, [ylow[a, i + DEPTH], mid, yhigh[a, i + DEPTH]])
            return c

        def upper(i, c):
            x = i + DEPTH + wide
            put(x, a, [ylow[a, x], high[a, i], yhigh[a, x]])
            return c

        lax.fori_loop(0, DEPTH, lower, 0)
        lax.fori_loop(0, wide, inner, 0)
        lax.fori_loop(0, DEPTH, upper, 0)


def thirds(v):
    hi = v.astype(jnp.bfloat16)
    rest = v - hi.astype(jnp.float32)
    mid = rest.astype(jnp.bfloat16)
    return hi, mid, (rest - mid.astype(jnp.float32)).astype(jnp.bfloat16)


def one_hot(cells, base, count):
    ids = lax.broadcasted_iota(jnp.int32, (count, cells.shape[1]), 0) + base
    return jnp.where(ids.astype(jnp.float32) == cells, 1.0, 0.0).astype(jnp.bfloat16)


def spread(hot, parts):
    total = jnp.dot(hot, parts[0], preferred_element_type=jnp.float32)
    total = total + jnp.dot(hot, parts[1], preferred_element_type=jnp.float32)
    return total + jnp.dot(hot, parts[2], preferred_element_type=jnp.float32)


def place_columns(cells, parts_ref, src, base, at, chunk, tall):
    hot = one_hot(cells, base * tall, chunk * tall)
    layers = src.shape[-1]
    for s in range(0, STEPS, 2):
        span = slice(s * layers, (s + 2) * layers)
        got = spread(hot, [parts_ref[n, :, span] for n in range(3)])
        for m in range(2):
            piece = got[:, m * layers : (m + 1) * layers]
            src[s + m, pl.ds(at, chunk)] = piece.reshape(chunk, tall, layers)


def source_ends_kernel(arrived, ends, first, last, cells_out, parts):
    block = 2 * STEPS + 1
    tiles = arrived.shape[0] // block
    half, tall, layers = ends.shape[1:]
    named = jnp.transpose(arrived[pl.ds(2 * STEPS, tiles, stride=block), :])
    cells = jnp.concatenate([named[0:1], named[1:2]], axis=1)
    cells_out[...] = jnp.broadcast_to(cells, cells_out.shape)
    for s in range(STEPS):
        for r in range(2):
            rows = pl.ds(r * STEPS + s, tiles, stride=block)
            for n, part in enumerate(thirds(arrived[rows, :])):
                parts[n, r * tiles : (r + 1) * tiles, s * layers : (s + 1) * layers] = part

    def body(i, c):
        place_columns(cells, parts, ends, i * (2 * half - DEPTH), i * DEPTH, DEPTH, tall)
        return c

    lax.fori_loop(0, 2, body, 0)
    for s in range(LAST):
        for d in range(1, LAST - s + 1):
            first[X_START[s] + d - 1] = ends[s, d - 1]
            last[X_START[s] + d - 1] = ends[s, half - d]


def source_middle_kernel(cells, parts, ends, middle, y_first, y_last):
    half, tall, _ = middle.shape[1:]

    def body(i, c):
        at = i * DEPTH
        place_columns(cells[:1], parts, middle, at + DEPTH, at, DEPTH, tall)
        return c

    lax.fori_loop(0, half // DEPTH, body, 0)
    for q in range(PAIRS):
        for out, at, is_first in ((y_first, 0, True), (y_last, tall - 8, False)):
            rows = slice(at, at + 8)
            for ref, begin, count, to in (
                (ends, 0, DEPTH, 0),
                (middle, 0, half, DEPTH),
                (ends, half - DEPTH, DEPTH, DEPTH + half),
            ):

                def inner(i, c):
                    for u in range(4):
                        x = i * 4 + u
                        far = ref[LAST - 1 - q, begin + x, rows, :] if q < PAIRS - 1 else None
                        out[q * 2 * half + to + x] = paired(
                            q, ref[q, begin + x, rows, :], far, is_first
                        )
                    return c

                lax.fori_loop(0, count // 4, inner, 0)


def paired(q, near, far, is_first):
    if far is None:
        return near
    row = lax.broadcasted_iota(jnp.int32, near.shape, 0)
    if is_first:
        return jnp.where(row <= LAST - 1 - q, near, pltpu.roll(far, LAST - q, 0))
    return jnp.where(row >= q + 1, near, pltpu.roll(far, q + 1, 0))


def corner_start(q):
    return sum(2 * Y_REACH[t] for t in range(q))


def source_corner_kernel(low, high, y_first, y_last):
    tall = low.shape[1]
    for q in range(PAIRS):
        far, reach, base = LAST - 1 - q, Y_REACH[q], corner_start(q)
        for out, at, is_first in ((y_first, 0, True), (y_last, tall - 8, False)):
            rows = slice(at, at + 8)
            for d in range(1, reach + 1):
                both = far != q and d <= q
                for halo, slot in ((low, base + reach - d), (high, base + reach + d - 1)):
                    a = halo[X_START[q] + d - 1, rows, :]
                    b = halo[X_START[far] + d - 1, rows, :] if both else None
                    out[slot] = paired(q, a, b, is_first)


def step_kernel(
    p0, vx0, vy0, vz0, bb, ss, ends, middle, low, high, ylow, yhigh, clow, chigh,
    p_out, vx_out, vy_out, vz_out, p, vx, vy, vz,
):
    wide, tall, layers = p_out.shape
    full = tall + 2 * DEPTH
    lane = lax.broadcasted_iota(jnp.int32, (full, layers), 1)
    blank = jnp.zeros((8, layers), jnp.float32)

    for s in range(STEPS):
        depth = LAST - s
        p_in, vx_in, vy_in, vz_in = (p0, vx0, vy0, vz0) if s == 0 else (p, vx, vy, vz)
        q = min(s, LAST - 1 - s)

        def tiles(x, corner=None):
            lo, hi = (ylow[q * wide + x], yhigh[q * wide + x]) if corner is None else (
                clow[corner_start(q) + Y_REACH[q] + corner],
                chigh[corner_start(q) + Y_REACH[q] + corner],
            )
            if s > LAST - 1 - s:
                lo, hi = pltpu.roll(lo, LAST - q, 0), pltpu.roll(hi, q + 1, 0)
            return lo, hi

        def row(i, carry, source):
            p_cur, vx_prev = carry
            p_next = p_in[i + 1]
            b = bb[i]
            vx_new = vx_in[i] - b * (p_next - p_cur)
            vy_new = vy_in[i] - b * (pltpu.roll(p_cur, full - 1, 0) - p_cur)
            up = jnp.where(lane == layers - 1, 0.0, pltpu.roll(p_cur, layers - 1, 1))
            vz_new = vz_in[i] - b * (up - p_cur)
            down = jnp.where(lane == 0, 0.0, pltpu.roll(vz_new, 1, 1))
            div = (vx_new - vx_prev) + (vy_new - pltpu.roll(vy_new, 1, 0)) + (vz_new - down)
            p_new = p_cur + ss[i] * (source - div)
            if s == LAST:
                keep = slice(DEPTH, DEPTH + tall)
                p_out[i - DEPTH] = p_new[keep]
                vx_out[i - DEPTH] = vx_new[keep]
                vy_out[i - DEPTH] = vy_new[keep]
                vz_out[i - DEPTH] = vz_new[keep]
            else:
                p[i] = p_new
                vx[i] = vx_new
                vy[i] = vy_new
                vz[i] = vz_new
            return p_next, vx_new

        begin = DEPTH - depth
        p_cur = p_in[begin]
        before = p_in[begin - 1]
        carry = (p_cur, vx_in[begin - 1] - bb[begin - 1] * (p_cur - before))
        for d in range(depth, 0, -1):
            lo, hi = tiles(0, -d) if d < depth else (blank, blank)
            source = jnp.concatenate([lo, low[X_START[s] + d - 1], hi], axis=0)
            carry = row(DEPTH - d, carry, source)

        half = wide // 2
        for ref, begin, count, to in (
            (ends, 0, DEPTH, 0),
            (middle, 0, half, DEPTH),
            (ends, half - DEPTH, DEPTH, DEPTH + half),
        ):

            def inner(n, carry):
                for u in range(4):
                    i = n * 4 + u
                    lo, hi = tiles(i + to) if s < LAST else (blank, blank)
                    source = jnp.concatenate([lo, ref[s, begin + i], hi], axis=0)
                    carry = row(i + to + DEPTH, carry, source)
                return carry

            carry = lax.fori_loop(0, count // 4, inner, carry)
        for d in range(1, depth + 1):
            lo, hi = tiles(0, d - 1) if d < depth else (blank, blank)
            source = jnp.concatenate([lo, high[X_START[s] + d - 1], hi], axis=0)
            carry = row(DEPTH + wide + d - 1, carry, source)


def program(
    pressure, vel_x, vel_y, vel_z, material, density_table, speed_table,
    panel_vals, panel_tile, panel_cell,
):
    devices = lax.axis_size("gx") * lax.axis_size("gy")
    wide, tall, layers = pressure.shape
    columns = panel_vals.shape[0] * panel_vals.shape[1]
    target = panel_tile.reshape(-1)
    order = jnp.arange(columns, dtype=jnp.int32)
    earlier = (target[:, None] == target[None, :]) & (order[None, :] < order[:, None])
    rank = jnp.sum(earlier.astype(jnp.int32), axis=1)
    values = panel_vals.reshape(columns, STEPS, layers)
    state = (pressure, vel_x, vel_y, vel_z, material)

    first, last = call(
        pack_kernel,
        [(5, DEPTH, tall, layers)] * 2,
        [pl.BlockSpec(memory_space=pltpu.HBM)] * 5,
        1,
        60,
        [pltpu.VMEM((2, DEPTH, tall, layers), jnp.int32), pltpu.SemaphoreType.DMA((5, 2))],
    )(*state)
    low, high = moved(last, "gx", 1), moved(first, "gx", -1)
    block = 2 * STEPS + 1
    (outgoing,) = call(
        send_kernel, [(devices * block, layers)], [SMEM] * 3 + [VMEM], 3, 12
    )(target, rank, panel_cell.reshape(-1), values)
    arrived = lax.all_to_all(
        outgoing.reshape(devices, block, 1, layers),
        ("gx", "gy"),
        split_axis=0,
        concat_axis=0,
        tiled=True,
    ).reshape(devices * block, layers)
    y_first, y_last = call(
        edge_kernel, [(5, wide + 2 * DEPTH, 8, layers)] * 2, [VMEM] * 7, 2, 12
    )(*state, low, high)
    y_low, y_high = moved(y_last, "gy", 1), moved(y_first, "gy", -1)
    b_table = courant * (1.0 / density_table)
    s_table = courant * (density_table * speed_table * speed_table)
    box = (wide + 2 * DEPTH, tall + 2 * DEPTH, layers)
    extended = call(extend_kernel, [box] * 6, [SMEM] * 2 + [VMEM] * 9, 4, 20)(
        b_table, s_table, *state, low, high, y_low, y_high
    )

    half = wide // 2
    parts_shape = jax.ShapeDtypeStruct((3, 2 * devices, STEPS * layers), jnp.bfloat16)
    ends, s_first, s_last, cells, parts = call(
        source_ends_kernel,
        [(STEPS, half, tall, layers)]
        + [(X_PLANES, tall, layers)] * 2
        + [(8, 2 * devices), parts_shape],
        [VMEM],
        3,
        26,
    )(arrived)
    s_low, s_high = moved(s_last, "gx", 1), moved(s_first, "gx", -1)
    middle, e_first, e_last = call(
        source_middle_kernel,
        [(STEPS, half, tall, layers)] + [(PAIRS * wide, 8, layers)] * 2,
        [VMEM] * 3,
        3,
        20,
    )(cells, parts, ends)
    e_low, e_high = moved(e_last, "gy", 1), moved(e_first, "gy", -1)
    c_first, c_last = call(
        source_corner_kernel, [(corner_start(PAIRS), 8, layers)] * 2, [VMEM] * 2, 1, 8
    )(s_low, s_high)
    c_low, c_high = moved(c_last, "gy", 1), moved(c_first, "gy", -1)

    return tuple(
        call(
            step_kernel,
            [(wide, tall, layers)] * 4,
            [VMEM] * 14,
            12,
            32,
            [pltpu.VMEM(box, jnp.float32)] * 4,
        )(*extended, ends, middle, s_low, s_high, e_low, e_high, c_low, c_high)
    )


def solution(mesh):
    tile = P("gx", "gy", None)
    return jax.shard_map(
        program,
        mesh=mesh,
        in_specs=(tile,) * 5
        + (
            P(),
            P(),
            P(("gx", "gy"), None, None, None),
            P(("gx", "gy"), None, None),
            P(("gx", "gy"), None),
        ),
        out_specs=(tile,) * 4,
        check_vma=False,
    )
```

```python
import functools

import jax
import jax.numpy as jnp
from jax import lax
from jax.experimental import pallas as pl
from jax.experimental.pallas import tpu as pltpu
from jax.sharding import PartitionSpec as P

courant = 0.55
STEPS = 8
DEPTH = 8
LAST = STEPS - 1
X_START = [sum(LAST - t for t in range(s)) for s in range(STEPS)]
X_PLANES = X_START[LAST]
PAIRS = 4
Y_REACH = [LAST - 1 - q for q in range(PAIRS)]
VMEM = pl.BlockSpec(memory_space=pltpu.VMEM)
SMEM = pl.BlockSpec(memory_space=pltpu.SMEM)


def call(kernel, outs, in_specs, micros, mib, scratch=()):
    return pl.pallas_call(
        kernel,
        out_shape=[
            shape
            if isinstance(shape, jax.ShapeDtypeStruct)
            else jax.ShapeDtypeStruct(shape, jnp.float32)
            for shape in outs
        ],
        in_specs=in_specs,
        out_specs=[VMEM] * len(outs),
        scratch_shapes=list(scratch),
        compiler_params=pltpu.CompilerParams(vmem_limit_bytes=mib << 20),
        cost_estimate=pl.CostEstimate(
            flops=0, transcendentals=0, bytes_accessed=int(micros * 2_000_000)
        ),
    )


def moved(block, axis, distance):
    devices = range(lax.axis_size(axis))
    route = [(i - distance, i) for i in devices if i - distance in devices]
    return lax.ppermute(block, axis, route)


def pack_kernel(p, vx, mat, vy, vz, first, last, first2, last2, ends, sems):
    wide = p.shape[0]
    copies = []
    for a, ref in enumerate((p, vx, mat, vy, vz)):
        late = a > 2
        deep = DEPTH - 1 if late else DEPTH
        for side, out in enumerate((first2, last2) if late else (first, last)):
            begin = (wide - deep) * side
            target = ends.at[side] if a == 2 else out.at[a - 3 if late else a]
            copies.append(
                pltpu.make_async_copy(ref.at[begin : begin + deep], target, sems.at[a, side])
            )
    for copy in copies:
        copy.start()
    for copy in copies:
        copy.wait()
    first[2] = ends[0].astype(jnp.float32) + 1.0
    last[2] = ends[1].astype(jnp.float32) + 1.0


def as_float(plane):
    return plane if plane.dtype == jnp.float32 else plane.astype(jnp.float32) + 1.0


def send_kernel(tile, rank, cell, vals, out):
    block = 2 * STEPS + 1
    tiles = out.shape[0] // block
    zero = jnp.zeros((16, out.shape[1]), jnp.float32)
    lane = lax.broadcasted_iota(jnp.int32, (1, out.shape[1]), 1)

    def clear(i, c):
        for u in range(4):
            out[pl.ds(pl.multiple_of(i * 64 + u * 16, 16), 16), :] = zero
        return c

    lax.fori_loop(0, out.shape[0] // 64, clear, 0)
    out[pl.ds(2 * STEPS, tiles, stride=block), :] = jnp.full((tiles, out.shape[1]), 65536.0)

    def place(i, c):
        for u in range(8):
            k = i * 8 + u
            at = tile[k] * block
            slot = rank[k]
            out[pl.ds(at + slot * STEPS, STEPS), :] = vals[k]
            named = out[pl.ds(at + 2 * STEPS, 1), :]
            own = cell[k].astype(jnp.float32)
            out[pl.ds(at + 2 * STEPS, 1), :] = jnp.where(lane == slot, own, named)
        return c

    lax.fori_loop(0, vals.shape[0] // 8, place, 0)


def edge_kernel(*refs):
    pack_edges(refs[:-4], *refs[-4:], 0)


def pack_edges(fields, low, high, first, last, base):
    wide, tall = fields[0].shape[:2]
    deep = low.shape[1]
    for a, ref in enumerate(fields):
        at = base + a * (wide + 2 * deep)
        for out, rows in ((first, slice(0, 8)), (last, slice(tall - 8, tall))):
            out[at : at + deep] = low[a, :, rows, :]
            out[at + deep : at + deep + wide] = as_float(ref[:, rows, :])
            out[at + deep + wide : at + wide + 2 * deep] = high[a, :, rows, :]


def extend(count, base, *refs):
    if len(refs) == 2 * count + 4:
        tables, fields = (), refs[:count]
        low, high, ylow, yhigh = refs[count : count + 4]
        outs = refs[count + 4 :]
    else:
        tables, fields = refs[:2], refs[2 : 2 + count]
        low, high, ylow, yhigh = refs[2 + count : 6 + count]
        outs = refs[6 + count :]
    wide = fields[0].shape[0]
    deep = low.shape[1]
    skip = DEPTH - deep

    def put(x, a, middle):
        at = base + a * (wide + 2 * deep) + x
        full = jnp.concatenate([ylow[at], middle, yhigh[at]], axis=0)
        if fields[a].dtype == jnp.float32:
            outs[a][x + skip] = full
            return
        btab, stab = tables
        b = jnp.zeros_like(full)
        s = jnp.zeros_like(full)
        for m in range(btab.shape[0]):
            b = jnp.where(full == float(m + 1), btab[m], b)
            s = jnp.where(full == float(m + 1), stab[m], s)
        outs[a][x + skip] = b
        outs[a + 1][x + skip] = s

    for a, ref in enumerate(fields):
        for i in range(deep):
            put(i, a, low[a, i])
            put(deep + wide + i, a, high[a, i])

        def inner(i, c):
            for u in range(2):
                put(i * 2 + u + deep, a, as_float(ref[i * 2 + u]))
            return c

        lax.fori_loop(0, wide // 2, inner, 0)


def thirds(v):
    hi = v.astype(jnp.bfloat16)
    rest = v - hi.astype(jnp.float32)
    mid = rest.astype(jnp.bfloat16)
    return hi, mid, (rest - mid.astype(jnp.float32)).astype(jnp.bfloat16)


def one_hot(cells, base, count):
    ids = lax.broadcasted_iota(jnp.int32, (count, cells.shape[1]), 0) + base
    return jnp.where(ids.astype(jnp.float32) == cells, 1.0, 0.0).astype(jnp.bfloat16)


def spread(hot, parts):
    total = jnp.dot(hot, parts[0], preferred_element_type=jnp.float32)
    total = total + jnp.dot(hot, parts[1], preferred_element_type=jnp.float32)
    return total + jnp.dot(hot, parts[2], preferred_element_type=jnp.float32)


def place_columns(cells, parts_ref, src, base, at, chunk, tall):
    hot = one_hot(cells, base * tall, chunk * tall)
    layers = src.shape[-1]
    for s in range(0, STEPS, 2):
        span = slice(s * layers, (s + 2) * layers)
        got = spread(hot, [parts_ref[n, :, span] for n in range(3)])
        for m in range(2):
            piece = got[:, m * layers : (m + 1) * layers]
            src[s + m, pl.ds(at, chunk)] = piece.reshape(chunk, tall, layers)


def source_ends_kernel(arrived, ends, first, last, cells_out, parts):
    block = 2 * STEPS + 1
    tiles = arrived.shape[0] // block
    half, tall, layers = ends.shape[1:]
    named = jnp.transpose(arrived[pl.ds(2 * STEPS, tiles, stride=block), :])
    cells = jnp.concatenate([named[0:1], named[1:2]], axis=1)
    cells_out[...] = jnp.broadcast_to(cells, cells_out.shape)
    for s in range(STEPS):
        for r in range(2):
            rows = pl.ds(r * STEPS + s, tiles, stride=block)
            for n, part in enumerate(thirds(arrived[rows, :])):
                parts[n, r * tiles : (r + 1) * tiles, s * layers : (s + 1) * layers] = part

    def body(i, c):
        place_columns(cells, parts, ends, i * (2 * half - DEPTH), i * DEPTH, DEPTH, tall)
        return c

    lax.fori_loop(0, 2, body, 0)
    for s in range(LAST):
        for d in range(1, LAST - s + 1):
            first[X_START[s] + d - 1] = ends[s, d - 1]
            last[X_START[s] + d - 1] = ends[s, half - d]


def source_middle_kernel(cells, parts, ends, vy, vz, low, high, middle, y_first, y_last):
    half, tall, _ = middle.shape[1:]
    pack_edges((vy, vz), low, high, y_first, y_last, PAIRS * 2 * half)

    def body(i, c):
        at = i * DEPTH
        place_columns(cells[:1], parts, middle, at + DEPTH, at, DEPTH, tall)
        return c

    lax.fori_loop(0, half // DEPTH, body, 0)
    for q in range(PAIRS):
        for out, at, is_first in ((y_first, 0, True), (y_last, tall - 8, False)):
            rows = slice(at, at + 8)
            for ref, begin, count, to in (
                (ends, 0, DEPTH, 0),
                (middle, 0, half, DEPTH),
                (ends, half - DEPTH, DEPTH, DEPTH + half),
            ):

                def inner(i, c):
                    for u in range(4):
                        x = i * 4 + u
                        far = ref[LAST - 1 - q, begin + x, rows, :] if q < PAIRS - 1 else None
                        out[q * 2 * half + to + x] = paired(
                            q, ref[q, begin + x, rows, :], far, is_first
                        )
                    return c

                lax.fori_loop(0, count // 4, inner, 0)


def paired(q, near, far, is_first):
    if far is None:
        return near
    row = lax.broadcasted_iota(jnp.int32, near.shape, 0)
    if is_first:
        return jnp.where(row <= LAST - 1 - q, near, pltpu.roll(far, LAST - q, 0))
    return jnp.where(row >= q + 1, near, pltpu.roll(far, q + 1, 0))


def corner_start(q):
    return sum(2 * Y_REACH[t] for t in range(q))


def source_corner_kernel(low, high, y_first, y_last):
    tall = low.shape[1]
    for q in range(PAIRS):
        far, reach, base = LAST - 1 - q, Y_REACH[q], corner_start(q)
        for out, at, is_first in ((y_first, 0, True), (y_last, tall - 8, False)):
            rows = slice(at, at + 8)
            for d in range(1, reach + 1):
                both = far != q and d <= q
                for halo, slot in ((low, base + reach - d), (high, base + reach + d - 1)):
                    a = halo[X_START[q] + d - 1, rows, :]
                    b = halo[X_START[far] + d - 1, rows, :] if both else None
                    out[slot] = paired(q, a, b, is_first)


def step_kernel(
    p0, vx0, vy0, vz0, bb, ss, ends, middle, low, high, ylow, yhigh, clow, chigh,
    p_out, vx_out, vy_out, vz_out, p, vx, vy, vz,
):
    wide, tall, layers = p_out.shape
    full = tall + 2 * DEPTH
    lane = lax.broadcasted_iota(jnp.int32, (full, layers), 1)
    blank = jnp.zeros((8, layers), jnp.float32)

    for s in range(STEPS):
        depth = LAST - s
        p_in, vx_in, vy_in, vz_in = (p0, vx0, vy0, vz0) if s == 0 else (p, vx, vy, vz)
        q = min(s, LAST - 1 - s)

        def tiles(x, corner=None):
            lo, hi = (ylow[q * wide + x], yhigh[q * wide + x]) if corner is None else (
                clow[corner_start(q) + Y_REACH[q] + corner],
                chigh[corner_start(q) + Y_REACH[q] + corner],
            )
            if s > LAST - 1 - s:
                lo, hi = pltpu.roll(lo, LAST - q, 0), pltpu.roll(hi, q + 1, 0)
            return lo, hi

        def row(i, carry, source):
            p_cur, vx_prev = carry
            p_next = p_in[i + 1]
            b = bb[i]
            vx_new = vx_in[i] - b * (p_next - p_cur)
            vy_new = vy_in[i] - b * (pltpu.roll(p_cur, full - 1, 0) - p_cur)
            up = jnp.where(lane == layers - 1, 0.0, pltpu.roll(p_cur, layers - 1, 1))
            vz_new = vz_in[i] - b * (up - p_cur)
            down = jnp.where(lane == 0, 0.0, pltpu.roll(vz_new, 1, 1))
            div = (vx_new - vx_prev) + (vy_new - pltpu.roll(vy_new, 1, 0)) + (vz_new - down)
            p_new = p_cur + ss[i] * (source - div)
            if s == LAST:
                keep = slice(DEPTH, DEPTH + tall)
                p_out[i - DEPTH] = p_new[keep]
                vx_out[i - DEPTH] = vx_new[keep]
                vy_out[i - DEPTH] = vy_new[keep]
                vz_out[i - DEPTH] = vz_new[keep]
            else:
                p[i] = p_new
                vx[i] = vx_new
                vy[i] = vy_new
                vz[i] = vz_new
            return p_next, vx_new

        begin = DEPTH - depth
        p_cur = p_in[begin]
        before = p_in[begin - 1]
        carry = (p_cur, vx_in[begin - 1] - bb[begin - 1] * (p_cur - before))
        for d in range(depth, 0, -1):
            lo, hi = tiles(0, -d) if d < depth else (blank, blank)
            source = jnp.concatenate([lo, low[X_START[s] + d - 1], hi], axis=0)
            carry = row(DEPTH - d, carry, source)

        half = wide // 2
        for ref, begin, count, to in (
            (ends, 0, DEPTH, 0),
            (middle, 0, half, DEPTH),
            (ends, half - DEPTH, DEPTH, DEPTH + half),
        ):

            def inner(n, carry):
                for u in range(4):
                    i = n * 4 + u
                    lo, hi = tiles(i + to) if s < LAST else (blank, blank)
                    source = jnp.concatenate([lo, ref[s, begin + i], hi], axis=0)
                    carry = row(i + to + DEPTH, carry, source)
                return carry

            carry = lax.fori_loop(0, count // 4, inner, carry)
        for d in range(1, depth + 1):
            lo, hi = tiles(0, d - 1) if d < depth else (blank, blank)
            source = jnp.concatenate([lo, high[X_START[s] + d - 1], hi], axis=0)
            carry = row(DEPTH + wide + d - 1, carry, source)


def program(
    pressure, vel_x, vel_y, vel_z, material, density_table, speed_table,
    panel_vals, panel_tile, panel_cell,
):
    devices = lax.axis_size("gx") * lax.axis_size("gy")
    wide, tall, layers = pressure.shape
    columns = panel_vals.shape[0] * panel_vals.shape[1]
    target = panel_tile.reshape(-1)
    order = jnp.arange(columns, dtype=jnp.int32)
    earlier = (target[:, None] == target[None, :]) & (order[None, :] < order[:, None])
    rank = jnp.sum(earlier.astype(jnp.int32), axis=1)
    values = panel_vals.reshape(columns, STEPS, layers)
    early, late = (pressure, vel_x, material), (vel_y, vel_z)
    hbm = pl.BlockSpec(memory_space=pltpu.HBM)
    first, last, first2, last2 = call(
        pack_kernel,
        [(3, DEPTH, tall, layers)] * 2 + [(2, DEPTH - 1, tall, layers)] * 2,
        [hbm] * 5,
        1,
        60,
        [pltpu.VMEM((2, DEPTH, tall, layers), jnp.int32), pltpu.SemaphoreType.DMA((5, 2))],
    )(*early, *late)
    low, high = moved(last, "gx", 1), moved(first, "gx", -1)
    low2, high2 = moved(last2, "gx", 1), moved(first2, "gx", -1)
    block = 2 * STEPS + 1
    (outgoing,) = call(
        send_kernel, [(devices * block, layers)], [SMEM] * 3 + [VMEM], 3, 12
    )(target, rank, panel_cell.reshape(-1), values)
    arrived = lax.all_to_all(
        outgoing.reshape(devices, block, 1, layers),
        ("gx", "gy"),
        split_axis=0,
        concat_axis=0,
        tiled=True,
    ).reshape(devices * block, layers)
    b_table = courant * (1.0 / density_table)
    s_table = courant * (density_table * speed_table * speed_table)
    box = (wide + 2 * DEPTH, tall + 2 * DEPTH, layers)

    tiles = len(early) * (wide + 2 * DEPTH)
    y_first, y_last = call(
        edge_kernel, [(tiles, 8, layers)] * 2, [VMEM] * 5, 2, 12
    )(*early, low, high)
    y_low, y_high = moved(y_last, "gy", 1), moved(y_first, "gy", -1)
    p_box, vx_box, b_box, s_box = call(
        functools.partial(extend, 3, 0), [box] * 4, [SMEM] * 2 + [VMEM] * 7, 3, 20
    )(b_table, s_table, *early, low, high, y_low, y_high)
    half = wide // 2
    parts_shape = jax.ShapeDtypeStruct((3, 2 * devices, STEPS * layers), jnp.bfloat16)
    ends, s_first, s_last, cells, parts = call(
        source_ends_kernel,
        [(STEPS, half, tall, layers)]
        + [(X_PLANES, tall, layers)] * 2
        + [(8, 2 * devices), parts_shape],
        [VMEM],
        3,
        26,
    )(arrived)
    s_low, s_high = moved(s_last, "gx", 1), moved(s_first, "gx", -1)
    middle, e_first, e_last = call(
        source_middle_kernel,
        [(STEPS, half, tall, layers)]
        + [(PAIRS * wide + len(late) * (wide + 2 * DEPTH - 2), 8, layers)] * 2,
        [VMEM] * 7,
        3,
        24,
    )(cells, parts, ends, *late, low2, high2)
    e_low, e_high = moved(e_last, "gy", 1), moved(e_first, "gy", -1)
    vy_box, vz_box = call(
        functools.partial(extend, 2, PAIRS * wide), [box] * 2, [VMEM] * 6, 2, 20
    )(*late, low2, high2, e_low, e_high)
    boxes = (p_box, vx_box, vy_box, vz_box, b_box, s_box)
    c_first, c_last = call(
        source_corner_kernel, [(corner_start(PAIRS), 8, layers)] * 2, [VMEM] * 2, 1, 8
    )(s_low, s_high)
    c_low, c_high = moved(c_last, "gy", 1), moved(c_first, "gy", -1)

    return tuple(
        call(
            step_kernel,
            [(wide, tall, layers)] * 4,
            [VMEM] * 14,
            12,
            32,
            [pltpu.VMEM(box, jnp.float32)] * 4,
        )(*boxes, ends, middle, s_low, s_high, e_low, e_high, c_low, c_high)
    )


def solution(mesh):
    tile = P("gx", "gy", None)
    return jax.shard_map(
        program,
        mesh=mesh,
        in_specs=(tile,) * 5
        + (
            P(),
            P(),
            P(("gx", "gy"), None, None, None),
            P(("gx", "gy"), None, None),
            P(("gx", "gy"), None),
        ),
        out_specs=(tile,) * 4,
        check_vma=False,
    )
```

```python
import functools

import jax
import jax.numpy as jnp
from jax import lax
from jax.experimental import pallas as pl
from jax.experimental.pallas import tpu as pltpu
from jax.sharding import PartitionSpec as P

courant = 0.55
STEPS = 8
DEPTH = 8
LAST = STEPS - 1
X_START = [sum(LAST - t for t in range(s)) for s in range(STEPS)]
X_PLANES = X_START[LAST]
PAIRS = 4
Y_REACH = [LAST - 1 - q for q in range(PAIRS)]
VMEM = pl.BlockSpec(memory_space=pltpu.VMEM)
SMEM = pl.BlockSpec(memory_space=pltpu.SMEM)


def call(kernel, outs, in_specs, micros, mib, scratch=(), out_spec=VMEM):
    return pl.pallas_call(
        kernel,
        out_shape=[
            shape
            if isinstance(shape, jax.ShapeDtypeStruct)
            else jax.ShapeDtypeStruct(shape, jnp.float32)
            for shape in outs
        ],
        in_specs=in_specs,
        out_specs=[out_spec] * len(outs),
        scratch_shapes=list(scratch),
        compiler_params=pltpu.CompilerParams(vmem_limit_bytes=mib << 20),
        cost_estimate=pl.CostEstimate(
            flops=0, transcendentals=0, bytes_accessed=int(micros * 2_000_000)
        ),
    )


def moved(block, axis, distance):
    devices = range(lax.axis_size(axis))
    route = [(i - distance, i) for i in devices if i - distance in devices]
    return lax.ppermute(block, axis, route)


def pack_kernel(p, vx, mat, vy, vz, first, last, first2, last2, ends, sems):
    wide = p.shape[0]
    copies = []
    for a, ref in enumerate((p, vx, mat, vy, vz)):
        late = a > 2
        deep = DEPTH - 1 if late else DEPTH
        for side, out in enumerate((first2, last2) if late else (first, last)):
            begin = (wide - deep) * side
            target = ends.at[side] if a == 2 else out.at[a - 3 if late else a]
            copies.append(
                pltpu.make_async_copy(ref.at[begin : begin + deep], target, sems.at[a, side])
            )
    for copy in copies:
        copy.start()
    for copy in copies:
        copy.wait()
    first[2] = ends[0].astype(jnp.float32) + 1.0
    last[2] = ends[1].astype(jnp.float32) + 1.0


def as_float(plane):
    return plane if plane.dtype == jnp.float32 else plane.astype(jnp.float32) + 1.0


def send_kernel(tile, rank, cell, vals, out):
    block = 2 * STEPS + 1
    tiles = out.shape[0] // block
    zero = jnp.zeros((16, out.shape[1]), jnp.float32)
    lane = lax.broadcasted_iota(jnp.int32, (1, out.shape[1]), 1)

    def clear(i, c):
        for u in range(4):
            out[pl.ds(pl.multiple_of(i * 64 + u * 16, 16), 16), :] = zero
        return c

    lax.fori_loop(0, out.shape[0] // 64, clear, 0)
    out[pl.ds(2 * STEPS, tiles, stride=block), :] = jnp.full((tiles, out.shape[1]), 65536.0)

    def place(i, c):
        for u in range(8):
            k = i * 8 + u
            at = tile[k] * block
            slot = rank[k]
            out[pl.ds(at + slot * STEPS, STEPS), :] = vals[k]
            named = out[pl.ds(at + 2 * STEPS, 1), :]
            own = cell[k].astype(jnp.float32)
            out[pl.ds(at + 2 * STEPS, 1), :] = jnp.where(lane == slot, own, named)
        return c

    lax.fori_loop(0, vals.shape[0] // 8, place, 0)


def edge_kernel(p, vx, mat, vy, vz, low, high, first, last):
    pack_edges((p, vx, mat), low, high, first, last, 0)
    wide, tall = vy.shape[:2]
    begin = 3 * (wide + 2 * DEPTH)
    for a, ref in enumerate((vy, vz)):
        rows = slice(begin + a * wide, begin + (a + 1) * wide)
        first[rows] = ref[:, :8, :]
        last[rows] = ref[:, tall - 8 :, :]


def pack_edges(fields, low, high, first, last, base):
    wide, tall = fields[0].shape[:2]
    deep = low.shape[1]
    for a, ref in enumerate(fields):
        at = base + a * (wide + 2 * deep)
        for out, rows in ((first, slice(0, 8)), (last, slice(tall - 8, tall))):
            out[at : at + deep] = low[a, :, rows, :]
            out[at + deep : at + deep + wide] = as_float(ref[:, rows, :])
            out[at + deep + wide : at + wide + 2 * deep] = high[a, :, rows, :]


def extend(count, base, *refs):
    if len(refs) == 2 * count + 4:
        tables, fields = (), refs[:count]
        low, high, ylow, yhigh = refs[count : count + 4]
        outs = refs[count + 4 :]
    else:
        tables, fields = refs[:2], refs[2 : 2 + count]
        low, high, ylow, yhigh = refs[2 + count : 6 + count]
        outs = refs[6 + count :]
    wide = fields[0].shape[0]
    deep = low.shape[1]
    skip = DEPTH - deep

    def put(x, a, middle):
        at = base + a * (wide + 2 * deep) + x
        full = jnp.concatenate([ylow[at], middle, yhigh[at]], axis=0)
        if fields[a].dtype == jnp.float32:
            outs[a][x + skip] = full
            return
        btab, stab = tables
        b = jnp.zeros_like(full)
        s = jnp.zeros_like(full)
        for m in range(btab.shape[0]):
            b = jnp.where(full == float(m + 1), btab[m], b)
            s = jnp.where(full == float(m + 1), stab[m], s)
        outs[a][x + skip] = b
        outs[a + 1][x + skip] = s

    for a, ref in enumerate(fields):
        for i in range(deep):
            put(i, a, low[a, i])
            put(deep + wide + i, a, high[a, i])

        def inner(i, c):
            for u in range(2):
                put(i * 2 + u + deep, a, as_float(ref[i * 2 + u]))
            return c

        lax.fori_loop(0, wide // 2, inner, 0)


def extend_late_kernel(vy, vz, low, high, ylow, yhigh, elow, ehigh, *outs):
    wide = vy.shape[0]
    deep = low.shape[1]
    for a, (ref, out) in enumerate(zip((vy, vz), outs)):
        main = 3 * (wide + 2 * DEPTH) + a * wide
        side = PAIRS * wide + 2 * a * deep
        for i in range(deep):
            k = side + i
            out[DEPTH - deep + i] = jnp.concatenate([elow[k], low[a, i], ehigh[k]], axis=0)
            k = side + deep + i
            out[DEPTH + wide + i] = jnp.concatenate([elow[k], high[a, i], ehigh[k]], axis=0)

        def inner(n, c):
            for u in range(2):
                i = n * 2 + u
                parts = [ylow[main + i], ref[i], yhigh[main + i]]
                out[i + DEPTH] = jnp.concatenate(parts, axis=0)
            return c

        lax.fori_loop(0, wide // 2, inner, 0)


def thirds(v):
    hi = v.astype(jnp.bfloat16)
    rest = v - hi.astype(jnp.float32)
    mid = rest.astype(jnp.bfloat16)
    return hi, mid, (rest - mid.astype(jnp.float32)).astype(jnp.bfloat16)


def one_hot(cells, base, count):
    ids = lax.broadcasted_iota(jnp.int32, (count, cells.shape[1]), 0) + base
    return jnp.where(ids.astype(jnp.float32) == cells, 1.0, 0.0).astype(jnp.bfloat16)


def spread(hot, parts):
    total = jnp.dot(hot, parts[0], preferred_element_type=jnp.float32)
    total = total + jnp.dot(hot, parts[1], preferred_element_type=jnp.float32)
    return total + jnp.dot(hot, parts[2], preferred_element_type=jnp.float32)


def place_columns(cells, parts_ref, src, base, at, chunk, tall):
    hot = one_hot(cells, base * tall, chunk * tall)
    layers = src.shape[-1]
    for s in range(0, STEPS, 2):
        span = slice(s * layers, (s + 2) * layers)
        got = spread(hot, [parts_ref[n, :, span] for n in range(3)])
        for m in range(2):
            piece = got[:, m * layers : (m + 1) * layers]
            src[s + m, pl.ds(at, chunk)] = piece.reshape(chunk, tall, layers)


def source_ends_kernel(arrived, ends, first, last, cells_out, parts):
    block = 2 * STEPS + 1
    tiles = arrived.shape[0] // block
    half, tall, layers = ends.shape[1:]
    named = jnp.transpose(arrived[pl.ds(2 * STEPS, tiles, stride=block), :])
    cells = jnp.concatenate([named[0:1], named[1:2]], axis=1)
    cells_out[...] = jnp.broadcast_to(cells, cells_out.shape)
    for s in range(STEPS):
        for r in range(2):
            rows = pl.ds(r * STEPS + s, tiles, stride=block)
            for n, part in enumerate(thirds(arrived[rows, :])):
                parts[n, r * tiles : (r + 1) * tiles, s * layers : (s + 1) * layers] = part

    def body(i, c):
        place_columns(cells, parts, ends, i * (2 * half - DEPTH), i * DEPTH, DEPTH, tall)
        return c

    lax.fori_loop(0, 2, body, 0)
    for s in range(LAST):
        for d in range(1, LAST - s + 1):
            first[X_START[s] + d - 1] = ends[s, d - 1]
            last[X_START[s] + d - 1] = ends[s, half - d]


def source_middle_kernel(cells, parts, ends, low, high, middle, y_first, y_last):
    half, tall, _ = middle.shape[1:]
    deep = low.shape[1]
    for a in range(low.shape[0]):
        for n, halo in enumerate((low, high)):
            begin = PAIRS * 2 * half + (2 * a + n) * deep
            y_first[begin : begin + deep] = halo[a, :, :8, :]
            y_last[begin : begin + deep] = halo[a, :, tall - 8 :, :]

    def body(i, c):
        at = i * DEPTH
        place_columns(cells[:1], parts, middle, at + DEPTH, at, DEPTH, tall)
        return c

    lax.fori_loop(0, half // DEPTH, body, 0)
    for q in range(PAIRS):
        for out, at, is_first in ((y_first, 0, True), (y_last, tall - 8, False)):
            rows = slice(at, at + 8)
            for ref, begin, count, to in (
                (ends, 0, DEPTH, 0),
                (middle, 0, half, DEPTH),
                (ends, half - DEPTH, DEPTH, DEPTH + half),
            ):

                def inner(i, c):
                    for u in range(4):
                        x = i * 4 + u
                        far = ref[LAST - 1 - q, begin + x, rows, :] if q < PAIRS - 1 else None
                        out[q * 2 * half + to + x] = paired(
                            q, ref[q, begin + x, rows, :], far, is_first
                        )
                    return c

                lax.fori_loop(0, count // 4, inner, 0)


def paired(q, near, far, is_first):
    if far is None:
        return near
    row = lax.broadcasted_iota(jnp.int32, near.shape, 0)
    if is_first:
        return jnp.where(row <= LAST - 1 - q, near, pltpu.roll(far, LAST - q, 0))
    return jnp.where(row >= q + 1, near, pltpu.roll(far, q + 1, 0))


def corner_start(q):
    return sum(2 * Y_REACH[t] for t in range(q))


def source_corner_kernel(low, high, y_first, y_last):
    tall = low.shape[1]
    for q in range(PAIRS):
        far, reach, base = LAST - 1 - q, Y_REACH[q], corner_start(q)
        for out, at, is_first in ((y_first, 0, True), (y_last, tall - 8, False)):
            rows = slice(at, at + 8)
            for d in range(1, reach + 1):
                both = far != q and d <= q
                for halo, slot in ((low, base + reach - d), (high, base + reach + d - 1)):
                    a = halo[X_START[q] + d - 1, rows, :]
                    b = halo[X_START[far] + d - 1, rows, :] if both else None
                    out[slot] = paired(q, a, b, is_first)


def step_kernel(
    p0, vx0, vy0, vz0, bb, ss, ends, middle, low, high, ylow, yhigh, clow, chigh,
    p_out, vx_out, vy_out, vz_out, p, vx, vy, vz, done, sems,
):
    wide, tall, layers = p_out.shape
    copies = []
    full = tall + 2 * DEPTH
    lane = lax.broadcasted_iota(jnp.int32, (full, layers), 1)
    blank = jnp.zeros((8, layers), jnp.float32)

    for s in range(STEPS):
        depth = LAST - s
        p_in, vx_in, vy_in, vz_in = (p0, vx0, vy0, vz0) if s == 0 else (p, vx, vy, vz)
        q = min(s, LAST - 1 - s)

        def tiles(x, corner=None):
            lo, hi = (ylow[q * wide + x], yhigh[q * wide + x]) if corner is None else (
                clow[corner_start(q) + Y_REACH[q] + corner],
                chigh[corner_start(q) + Y_REACH[q] + corner],
            )
            if s > LAST - 1 - s:
                lo, hi = pltpu.roll(lo, LAST - q, 0), pltpu.roll(hi, q + 1, 0)
            return lo, hi

        def row(i, carry, source):
            p_cur, vx_prev = carry
            p_next = p_in[i + 1]
            b = bb[i]
            vx_new = vx_in[i] - b * (p_next - p_cur)
            vy_new = vy_in[i] - b * (pltpu.roll(p_cur, full - 1, 0) - p_cur)
            up = jnp.where(lane == layers - 1, 0.0, pltpu.roll(p_cur, layers - 1, 1))
            vz_new = vz_in[i] - b * (up - p_cur)
            down = jnp.where(lane == 0, 0.0, pltpu.roll(vz_new, 1, 1))
            div = (vx_new - vx_prev) + (vy_new - pltpu.roll(vy_new, 1, 0)) + (vz_new - down)
            p_new = p_cur + ss[i] * (source - div)
            if s == LAST:
                keep = slice(DEPTH, DEPTH + tall)
                for a, new in enumerate((p_new, vx_new, vy_new, vz_new)):
                    done[a, i - DEPTH] = new[keep]
            else:
                p[i] = p_new
                vx[i] = vx_new
                vy[i] = vy_new
                vz[i] = vz_new
            return p_next, vx_new

        begin = DEPTH - depth
        p_cur = p_in[begin]
        before = p_in[begin - 1]
        carry = (p_cur, vx_in[begin - 1] - bb[begin - 1] * (p_cur - before))
        for d in range(depth, 0, -1):
            lo, hi = tiles(0, -d) if d < depth else (blank, blank)
            source = jnp.concatenate([lo, low[X_START[s] + d - 1], hi], axis=0)
            carry = row(DEPTH - d, carry, source)

        half = wide // 2
        for ref, begin, count, to in (
            (ends, 0, DEPTH, 0),
            (middle, 0, half, DEPTH),
            (ends, half - DEPTH, DEPTH, DEPTH + half),
        ):

            def inner(n, carry):
                for u in range(8):
                    i = n * 8 + u
                    lo, hi = tiles(i + to) if s < LAST else (blank, blank)
                    source = jnp.concatenate([lo, ref[s, begin + i], hi], axis=0)
                    carry = row(i + to + DEPTH, carry, source)
                return carry

            carry = lax.fori_loop(0, count // 8, inner, carry)
            if s == LAST:
                rows = pl.ds(to, count)
                for a, out in enumerate((p_out, vx_out, vy_out, vz_out)):
                    sem = sems.at[a, len(copies) // 4]
                    copies.append(pltpu.make_async_copy(done.at[a, rows], out.at[rows], sem))
                    copies[-1].start()
        for d in range(1, depth + 1):
            lo, hi = tiles(0, d - 1) if d < depth else (blank, blank)
            source = jnp.concatenate([lo, high[X_START[s] + d - 1], hi], axis=0)
            carry = row(DEPTH + wide + d - 1, carry, source)
    for copy in copies:
        copy.wait()


def program(
    pressure, vel_x, vel_y, vel_z, material, density_table, speed_table,
    panel_vals, panel_tile, panel_cell,
):
    devices = lax.axis_size("gx") * lax.axis_size("gy")
    wide, tall, layers = pressure.shape
    columns = panel_vals.shape[0] * panel_vals.shape[1]
    target = panel_tile.reshape(-1)
    order = jnp.arange(columns, dtype=jnp.int32)
    earlier = (target[:, None] == target[None, :]) & (order[None, :] < order[:, None])
    rank = jnp.sum(earlier.astype(jnp.int32), axis=1)
    values = panel_vals.reshape(columns, STEPS, layers)
    early, late = (pressure, vel_x, material), (vel_y, vel_z)
    hbm = pl.BlockSpec(memory_space=pltpu.HBM)
    first, last, first2, last2 = call(
        pack_kernel,
        [(3, DEPTH, tall, layers)] * 2 + [(2, DEPTH - 1, tall, layers)] * 2,
        [hbm] * 5,
        1,
        60,
        [pltpu.VMEM((2, DEPTH, tall, layers), jnp.int32), pltpu.SemaphoreType.DMA((5, 2))],
    )(*early, *late)
    low, high = moved(last, "gx", 1), moved(first, "gx", -1)
    low2, high2 = moved(last2, "gx", 1), moved(first2, "gx", -1)
    block = 2 * STEPS + 1
    (outgoing,) = call(
        send_kernel, [(devices * block, layers)], [SMEM] * 3 + [VMEM], 3, 12
    )(target, rank, panel_cell.reshape(-1), values)
    arrived = lax.all_to_all(
        outgoing.reshape(devices, block, 1, layers),
        ("gx", "gy"),
        split_axis=0,
        concat_axis=0,
        tiled=True,
    ).reshape(devices * block, layers)
    b_table = courant * (1.0 / density_table)
    s_table = courant * (density_table * speed_table * speed_table)
    box = (wide + 2 * DEPTH, tall + 2 * DEPTH, layers)

    tiles = 3 * (wide + 2 * DEPTH) + 2 * wide
    y_first, y_last = call(
        edge_kernel, [(tiles, 8, layers)] * 2, [VMEM] * 7, 2, 14
    )(*early, *late, low, high)
    y_low, y_high = moved(y_last, "gy", 1), moved(y_first, "gy", -1)
    p_box, vx_box, b_box, s_box = call(
        functools.partial(extend, 3, 0), [box] * 4, [SMEM] * 2 + [VMEM] * 7, 3, 20
    )(b_table, s_table, *early, low, high, y_low, y_high)
    half = wide // 2
    parts_shape = jax.ShapeDtypeStruct((3, 2 * devices, STEPS * layers), jnp.bfloat16)
    ends, s_first, s_last, cells, parts = call(
        source_ends_kernel,
        [(STEPS, half, tall, layers)]
        + [(X_PLANES, tall, layers)] * 2
        + [(8, 2 * devices), parts_shape],
        [VMEM],
        3,
        26,
    )(arrived)
    s_low, s_high = moved(s_last, "gx", 1), moved(s_first, "gx", -1)
    middle, e_first, e_last = call(
        source_middle_kernel,
        [(STEPS, half, tall, layers)]
        + [(PAIRS * wide + 4 * (DEPTH - 1), 8, layers)] * 2,
        [VMEM] * 5,
        3,
        24,
    )(cells, parts, ends, low2, high2)
    e_low, e_high = moved(e_last, "gy", 1), moved(e_first, "gy", -1)
    vy_box, vz_box = call(
        extend_late_kernel, [box] * 2, [VMEM] * 8, 2, 20
    )(*late, low2, high2, y_low, y_high, e_low, e_high)
    boxes = (p_box, vx_box, vy_box, vz_box, b_box, s_box)
    c_first, c_last = call(
        source_corner_kernel, [(corner_start(PAIRS), 8, layers)] * 2, [VMEM] * 2, 1, 8
    )(s_low, s_high)
    c_low, c_high = moved(c_last, "gy", 1), moved(c_first, "gy", -1)

    return tuple(
        call(
            step_kernel,
            [(wide, tall, layers)] * 4,
            [VMEM] * 14,
            12,
            32,
            [pltpu.VMEM(box, jnp.float32)] * 4
            + [pltpu.VMEM((4, wide, tall, layers), jnp.float32), pltpu.SemaphoreType.DMA((4, 3))],
            hbm,
        )(*boxes, ends, middle, s_low, s_high, e_low, e_high, c_low, c_high)
    )


def solution(mesh):
    tile = P("gx", "gy", None)
    return jax.shard_map(
        program,
        mesh=mesh,
        in_specs=(tile,) * 5
        + (
            P(),
            P(),
            P(("gx", "gy"), None, None, None),
            P(("gx", "gy"), None, None),
            P(("gx", "gy"), None),
        ),
        out_specs=(tile,) * 4,
        check_vma=False,
    )
```
